32 devices in a mesh: fsdp: 32 (over z, y, x, core).
Axes of the slice: x: 2, y: 2, z: 4, core: 2. Of those that a mesh axis runs over, the one named last changes fastest.
Arguments:
- block_in: bfloat16 [8192, 768], P('fsdp'), may hold values from -6 to 6
- segment_ids: int32 [8192], P('fsdp'), may hold values from 0 to 8191, as said below
- live_count: int32 [32], P('fsdp'), may hold values from 128 to 256, as said below
- norm_gain: bfloat16 [768], P('fsdp'), may hold values from 0.099609375 to 1.8984375
- in_weight: bfloat16 [768, 3352], P('fsdp'), may hold values from -0.21875 to 0.21875
- conv_weight: bfloat16 [1792, 4], P('fsdp'), may hold values from -3 to 3
- conv_bias: bfloat16 [1792], P('fsdp'), may hold values from -3 to 3
- step_bias: float32 [24], replicated, may hold values from -6 to -3
- decay_log: float32 [24], replicated, may hold values from 0 to 2.5
- skip_gain: float32 [24], replicated, may hold values from 0.5 to 1.5
- gated_gain: bfloat16 [1536], P('fsdp'), may hold values from 0.099609375 to 1.8984375
- out_weight: bfloat16 [1536, 768], P('fsdp'), may hold values from -0.15625 to 0.15625
- out_cotangent: bfloat16 [8192, 768], P('fsdp'), may hold values from -6 to 6
Outputs:
- block_out: bfloat16 [8192, 768], P('fsdp')
- input_grad: float32 [8192, 768], P('fsdp')
- norm_gain_grad: float32 [768], P('fsdp')
- in_weight_grad: float32 [768, 3352], P('fsdp')
- conv_weight_grad: float32 [1792, 4], P('fsdp')
- conv_bias_grad: float32 [1792], P('fsdp')
- step_bias_grad: float32 [24], replicated
- decay_log_grad: float32 [24], replicated
- skip_gain_grad: float32 [24], replicated
- gated_gain_grad: float32 [1536], P('fsdp')
- out_weight_grad: float32 [1536, 768], P('fsdp')
The draws below stay inside these ranges and needn't reach their ends.
Inputs may be any that keep to these rules, and one draw needn't show every extreme that they name: `segment_ids`: segment numbers never fall inside a device's 256 slots and no segment spans two devices; a segment holds 1 to 256 slots and one holds exactly 256; a device's first padding slot starts a new segment. `live_count`: live slots come first in each device's 256 slots; one device is full in every draw.
All inputs are finite; a program needn't handle non-finite values.
Results may differ from the reference program's by a relative error of at most 0.0098.
Values may be sent and summed in bfloat16 or wider, within the bound.
A program may use at most 128 MiB of HBM per device.

```python
from functools import partial
import jax
import jax.numpy as jnp
from jax import lax

D = 768
DI = 1536
STATE = 128
HDIM = 64
KCONV = 4
SCAN_BLOCK = 128
TOK_DEV = 256
HEADS = 24
SEQMAX = 256
CONV = 1792
PROJ = 3352
TOKENS = 8192
N_FSDP = 32


def layout_draw(key):
    full_dev = jax.random.randint(jax.random.fold_in(key, 11), (), 0, N_FSDP)
    counts = jax.random.randint(jax.random.fold_in(key, 12), (N_FSDP,), TOK_DEV // 2, TOK_DEV + 1)
    device_ids = jnp.arange(N_FSDP, dtype=jnp.int32)
    counts = jnp.where(device_ids == full_dev, TOK_DEV, counts).astype(jnp.int32)
    slot_index = jnp.arange(TOK_DEV, dtype=jnp.int32)
    coin_draws = jax.random.randint(jax.random.fold_in(key, 13), (N_FSDP, TOK_DEV), 0, SEQMAX)
    protected = (device_ids[:, None] == full_dev) & (slot_index[None, :] < SEQMAX)
    starts = (slot_index[None, :] % SEQMAX == 0) | (slot_index[None, :] == counts[:, None]) | (coin_draws < 3) & jnp.logical_not(protected)
    segment_num = jnp.cumsum(starts.astype(jnp.int32), axis=1) - 1 + device_ids[:, None] * TOK_DEV
    return (counts, segment_num.reshape(-1).astype(jnp.int32))


def draw_live_count(key, part):
    return layout_draw(key)[0]


def draw_segment_ids(key, part):
    return layout_draw(key)[1]


def levels(key, dims, shards, smallest, largest):
    def one(position, parts):
        heights = jax.random.uniform(jax.random.fold_in(jax.random.fold_in(key, 6), position), (parts,), jnp.float32, smallest / len(shards), largest / len(shards))
        return jnp.repeat(jnp.exp(heights), dims[position] // parts).reshape((-1,) + (1,) * (len(dims) - position - 1))

    level = one(*shards[0])
    for cut in shards[1:]:
        level = level * one(*cut)
    return level


def bell_draw(rng, dims, scale, most, cuts=(), kind=jnp.bfloat16):
    entries = jax.random.normal(rng, dims, jnp.float32) * scale
    if len(cuts) > 0:
        entries = levels(rng, dims, cuts, -0.22, 0.18) * entries
    return jnp.clip(entries, min=-most, max=most).astype(kind)


def setup_inputs(seed: int = 0) -> dict:
    splits = jax.random.split(jax.random.key(seed), 14)
    return {
        "block_in": bell_draw(splits[0], (TOKENS, D), 1.0, 6.0, ((0, 32),)),
        "segment_ids": draw_segment_ids(jax.random.fold_in(splits[13], 71), 0),
        "live_count": draw_live_count(jax.random.fold_in(splits[13], 71), 0),
        "norm_gain": jnp.clip(1.0 + 0.18 * jax.random.normal(splits[3], (D,), jnp.float32), 0.099609375, 1.8984375).astype(jnp.bfloat16),
        "in_weight": bell_draw(splits[4], (D, PROJ), D ** -0.5, 0.21875, ((0, 32),)),
        "conv_weight": bell_draw(splits[5], (CONV, KCONV), KCONV ** -0.5, 3.0, ((0, 32),)),
        "conv_bias": bell_draw(splits[6], (CONV,), 0.5, 3.0, ((0, 32),)),
        "step_bias": jnp.clip(jax.random.uniform(splits[7], (HEADS,), jnp.float32, -6.0, -3.0), -6.0, -3.0),
        "decay_log": jnp.clip(jax.random.uniform(splits[8], (HEADS,), jnp.float32, 0.0, 2.5), 0.0, 2.5),
        "skip_gain": jnp.clip(jax.random.uniform(splits[9], (HEADS,), jnp.float32, 0.5, 1.5), 0.5, 1.5),
        "gated_gain": jnp.clip(1.0 + 0.18 * jax.random.normal(splits[10], (DI,), jnp.float32), 0.099609375, 1.8984375).astype(jnp.bfloat16),
        "out_weight": bell_draw(splits[11], (DI, D), DI ** -0.5, 0.15625, ((0, 32),)),
        "out_cotangent": bell_draw(splits[12], (TOKENS, D), 1.0, 6.0, ((0, 32),)),
    }


EPSILON = 1e-05
HIGHEST = lax.Precision.HIGHEST

def rms_scale(values, gain_vec):
    return values * lax.rsqrt(lax.optimization_barrier(jnp.mean(values * values, axis=-1, keepdims=True)) + EPSILON) * gain_vec

def convolve(inputs, kernel_w, kernel_bias, segments):
    length = inputs.shape[0]
    conv_total = kernel_bias[None, :] + kernel_w[:, KCONV - 1][None, :] * inputs
    for offset in range(1, KCONV):
        moved_in = jnp.concatenate([jnp.zeros((offset, inputs.shape[1]), inputs.dtype), inputs[:length - offset]], axis=0)
        earlier = jnp.concatenate([jnp.full((offset,), -1, jnp.int32), segments[:length - offset]], axis=0)
        same_seg = (earlier == segments).astype(inputs.dtype)
        conv_total = conv_total + kernel_w[:, KCONV - 1 - offset][None, :] * moved_in * same_seg[:, None]
    return conv_total

def block_step(carry_state, pieces):
    values, keys_in, queries, step_sizes, logdecay, group_segs, before = pieces
    positions = jnp.arange(SCAN_BLOCK)
    lower_mask = positions[:, None] >= positions[None, :]
    running = jnp.dot(lower_mask.astype(logdecay.dtype), logdecay, precision=HIGHEST)
    same_seg = lower_mask & (group_segs[:, None] == group_segs[None, :])
    spread = running.T[:, :, None] - running.T[:, None, :]
    decay_mat = jnp.where(same_seg[None], jnp.exp(jnp.where(same_seg[None], spread, 0.0)), 0.0)
    intersection = jnp.dot(queries, keys_in.T, precision=HIGHEST)
    weights_all = decay_mat * intersection[None] * step_sizes.T[:, None, :]
    intra_out = jnp.einsum('hts,shp->thp', weights_all, values, precision=HIGHEST)
    carried = (group_segs == before).astype(logdecay.dtype)
    factor = carried[:, None] * jnp.exp(running)
    inter_out = jnp.einsum('tn,hpn->thp', queries, carry_state, precision=HIGHEST) * factor[:, :, None]
    tail_mask = (group_segs == group_segs[-1]).astype(logdecay.dtype)
    towards = jnp.exp(running[-1][None, :] - running) * tail_mask[:, None] * step_sizes
    fresh_state = jnp.einsum('shp,sn->hpn', towards[:, :, None] * values, keys_in, precision=HIGHEST)
    new_state = fresh_state + (carried[-1] * jnp.exp(running[-1]))[:, None, None] * carry_state
    return (new_state, intra_out + inter_out)

def run_mixer(segments, projected, params):
    kernel_w, kernel_bias, bias_step, log_rate, skip_vec, gain_gated = params
    length = projected.shape[0]
    gating = projected[:, :DI]
    conv_in = projected[:, DI:DI + CONV]
    raw_step = projected[:, DI + CONV:]
    activated = jax.nn.silu(convolve(conv_in, kernel_w, kernel_bias, segments))
    values = activated[:, :DI].reshape(length, HEADS, HDIM)
    keys_in = activated[:, DI:DI + STATE]
    queries = activated[:, DI + STATE:]
    step_sizes = jax.nn.softplus(raw_step + bias_step[None, :])
    logdecay = -step_sizes * jnp.exp(log_rate)[None, :]
    block_count = length // SCAN_BLOCK
    group_segs = segments.reshape(block_count, SCAN_BLOCK)
    before = jnp.concatenate([jnp.full((1,), -1, jnp.int32), group_segs[:-1, -1]])
    pieces = (values.reshape(block_count, SCAN_BLOCK, HEADS, HDIM), keys_in.reshape(block_count, SCAN_BLOCK, STATE), queries.reshape(block_count, SCAN_BLOCK, STATE), step_sizes.reshape(block_count, SCAN_BLOCK, HEADS), logdecay.reshape(block_count, SCAN_BLOCK, HEADS), group_segs, before)
    initial_state = jnp.zeros((HEADS, HDIM, STATE), projected.dtype)
    _, outputs = lax.scan(jax.checkpoint(block_step), initial_state, pieces)
    scanned = outputs.reshape(length, HEADS, HDIM) + skip_vec[None, :, None] * values
    gated = scanned.reshape(length, DI) * jax.nn.silu(gating)
    return rms_scale(gated, gain_gated)

def block_pass(weights, inputs, segments, live_total, cotangent):
    in_full, out_full, gain_norm, params = weights
    source = inputs.astype(jnp.float32)
    live_rows = (jnp.arange(TOK_DEV) < live_total).astype(jnp.float32)
    normed = rms_scale(source, gain_norm).astype(jnp.bfloat16)
    projected = jnp.dot(normed, in_full, preferred_element_type=jnp.float32)
    mixer_out, mixer_vjp = jax.vjp(partial(run_mixer, segments), projected, params)
    mixer_low = mixer_out.astype(jnp.bfloat16)
    branch = jnp.dot(mixer_low, out_full, preferred_element_type=jnp.float32)
    output = (source + live_rows[:, None] * branch).astype(jnp.bfloat16)
    masked = jnp.where(live_rows[:, None] > 0, cotangent, jnp.zeros_like(cotangent))
    grad_out_w = jnp.dot(mixer_low.T, masked, preferred_element_type=jnp.float32)
    grad_mixer = jnp.dot(masked, out_full.T, preferred_element_type=jnp.float32)
    grad_proj, grad_params = mixer_vjp(grad_mixer)
    grad_low = grad_proj.astype(jnp.bfloat16)
    grad_in_w = jnp.dot(normed.T, grad_low, preferred_element_type=jnp.float32)
    grad_normed = jnp.dot(grad_low, in_full.T, preferred_element_type=jnp.float32)
    _, norm_vjp = jax.vjp(rms_scale, source, gain_norm)
    grad_source, grad_gain = norm_vjp(grad_normed)
    grad_input = cotangent.astype(jnp.float32) + grad_source
    return (output, grad_input, (grad_gain, grad_in_w, grad_params, grad_out_w))

def reference(block_in, segment_ids, live_count, norm_gain, in_weight, conv_weight, conv_bias, step_bias, decay_log, skip_gain, gated_gain, out_weight, out_cotangent):
    params = (conv_weight.astype(jnp.float32), conv_bias.astype(jnp.float32), step_bias, decay_log, skip_gain, gated_gain.astype(jnp.float32))
    weights = (in_weight, out_weight, norm_gain.astype(jnp.float32), params)

    def per_block(totals, block_items):
        output, grad_input, grads = block_pass(weights, *block_items)
        return (jax.tree.map(jnp.add, totals, grads), (output, grad_input))
    initial = (jnp.zeros((D,), jnp.float32), jnp.zeros((D, PROJ), jnp.float32), jax.tree.map(jnp.zeros_like, params), jnp.zeros((DI, D), jnp.float32))
    block_items = (block_in.reshape(N_FSDP, TOK_DEV, D), segment_ids.reshape(N_FSDP, TOK_DEV), live_count, out_cotangent.reshape(N_FSDP, TOK_DEV, D))
    totals, results = lax.scan(per_block, initial, block_items)
    gain_grad, in_grad, param_grads, out_grad = totals
    outputs, grad_inputs = results
    return (outputs.reshape(TOKENS, D), grad_inputs.reshape(TOKENS, D), gain_grad, in_grad, param_grads[0], param_grads[1], param_grads[2], param_grads[3], param_grads[4], param_grads[5], out_grad)
```

```python
import functools

import jax
import jax.numpy as jnp
from jax import lax
from jax.experimental import pallas as pl
from jax.experimental.pallas import tpu as pltpu
from jax.sharding import PartitionSpec as P

DI = 1536
STATE = 128
HDIM = 64
KCONV = 4
HEADS = 24
CONV = 1792
LANES = 128
EPSILON = 1e-05
HIGHEST = lax.Precision.HIGHEST
F32 = jnp.float32
BF16 = jnp.bfloat16
NT = (((1,), (1,)), ((), ()))
TN = (((0,), (0,)), ((), ()))


def rms_scale(values, gain_vec):
    return (
        values * lax.rsqrt(jnp.mean(values * values, axis=-1, keepdims=True) + EPSILON) * gain_vec
    )


def dot(a, b, dims=(((1,), (0,)), ((), ()))):
    return lax.dot_general(a.astype(BF16), b.astype(BF16), dims, preferred_element_type=F32)


def sigmoid(v):
    return 1.0 / (1.0 + jnp.exp(-v))


def softplus(v):
    return jnp.maximum(v, 0.0) + jnp.log1p(jnp.exp(-jnp.abs(v)))


def chunk_ds(i):
    return pl.ds(pl.multiple_of(i * LANES, LANES), LANES)


def head_prelude(raw_ref, segc, segr, bias_ref, rate_ref):
    length = raw_ref.shape[0]
    rows = lax.broadcasted_iota(jnp.int32, (length, length), 0)
    cols = lax.broadcasted_iota(jnp.int32, (length, length), 1)
    mask = ((rows >= cols) & (segc == segr)).astype(F32)
    shifted = raw_ref[...] + bias_ref[...]
    step = softplus(shifted)
    decay = -step * rate_ref[...]
    running = jnp.dot(mask, decay, precision=HIGHEST, preferred_element_type=F32)
    return mask, shifted, step, decay, running


def column(values, h):
    lane = lax.broadcasted_iota(jnp.int32, values.shape, 1)
    return jnp.sum(jnp.where(lane == h, values, 0.0), axis=1, keepdims=True)


def decay_of(mask_ref, run_ref, run_t_ref, h):
    spread = column(run_ref[...], h) - run_t_ref[pl.ds(h, 1), :]
    mask = mask_ref[...]
    return jnp.where(mask > 0, jnp.exp(jnp.where(mask > 0, spread, 0.0)), 0.0)


def forward_kernel(
    proj_ref, raw_ref, segc_ref, segr_ref, shift_ref, cw_ref, bias_ref, rate_ref, skip_ref, gain_ref,
    pre_ref, scan_ref, low_ref,
    mask_s, run_s, runt_s, stept_s, inter_s, gated_s,
):
    length = proj_ref.shape[0]
    mask, _, step, _, running = head_prelude(
        raw_ref, segc_ref[...], segr_ref[...], bias_ref, rate_ref
    )
    mask_s[...] = mask
    run_s[...] = running
    runt_s[...] = running.T
    stept_s[...] = step.T

    def conv(i, _):
        ds = chunk_ds(i)
        x = proj_ref[:, chunk_ds(i + DI // LANES)]
        total = cw_ref[KCONV : KCONV + 1, ds] + cw_ref[KCONV - 1 : KCONV, ds] * x
        for j in range(1, KCONV):
            moved = pltpu.roll(x, j, 0) * shift_ref[:, j - 1 : j]
            total = total + cw_ref[KCONV - 1 - j : KCONV - j, ds] * moved
        pre_ref[:, ds] = total
        return 0

    lax.fori_loop(0, CONV // LANES, conv, 0)
    pre_k = pre_ref[:, DI : DI + STATE]
    pre_q = pre_ref[:, DI + STATE :]
    inter_s[...] = dot(pre_q * sigmoid(pre_q), pre_k * sigmoid(pre_k), NT)

    def pair(i, sumsq):
        ds = chunk_ds(i)
        pre = pre_ref[:, ds]
        values = pre * sigmoid(pre)
        low = values.astype(BF16)
        outs = []
        for side in range(2):
            h = 2 * i + side
            weights = decay_of(mask_s, run_s, runt_s, h) * inter_s[...] * stept_s[pl.ds(h, 1), :]
            outs.append(dot(weights, low))
        lane = lax.broadcasted_iota(jnp.int32, (length, LANES), 1)
        scanned = jnp.where(lane < HDIM, outs[0], outs[1]) + skip_ref[:, ds] * values
        scan_ref[:, ds] = scanned
        z = proj_ref[:, ds]
        gated = scanned * (z * sigmoid(z))
        gated_s[:, ds] = gated
        return sumsq + gated * gated

    sumsq = lax.fori_loop(0, DI // LANES, pair, jnp.zeros((length, LANES), F32))
    scale = lax.rsqrt(jnp.sum(sumsq, axis=1, keepdims=True) / DI + EPSILON)

    def finish(i, _):
        ds = chunk_ds(i)
        low_ref[:, ds] = (gated_s[:, ds] * scale * gain_ref[:, ds]).astype(BF16)
        return 0

    lax.fori_loop(0, DI // LANES, finish, 0)


def backward_kernel(
    proj_ref, raw_ref, segc_ref, segr_ref, shift_ref, cw_ref, bias_ref, rate_ref, skip_ref, gain_ref,
    pre_ref, scan_ref, gm_ref,
    glow_ref, graw_ref, gconv_ref, gdi_ref, ghead_ref,
    mask_s, run_s, runt_s, stept_s, inter_s, dinter_s, row_s, col_s,
):
    length = proj_ref.shape[0]
    mask, shifted, step, decay, running = head_prelude(
        raw_ref, segc_ref[...], segr_ref[...], bias_ref, rate_ref
    )
    mask_s[...] = mask
    run_s[...] = running
    runt_s[...] = running.T
    stept_s[...] = step.T
    pre_k = pre_ref[:, DI : DI + STATE]
    pre_q = pre_ref[:, DI + STATE :]
    keys = (pre_k * sigmoid(pre_k)).astype(BF16)
    queries = (pre_q * sigmoid(pre_q)).astype(BF16)
    inter_s[...] = dot(queries, keys, NT)
    dinter_s[...] = jnp.zeros_like(dinter_s)
    row_s[...] = jnp.zeros_like(row_s)
    col_s[...] = jnp.zeros_like(col_s)
    gconv_ref[...] = jnp.zeros_like(gconv_ref)
    gdi_ref[...] = jnp.zeros_like(gdi_ref)
    ghead_ref[...] = jnp.zeros_like(ghead_ref)

    def sums(i, carry):
        sumsq, inner = carry
        ds = chunk_ds(i)
        z = proj_ref[:, ds]
        gated = scan_ref[:, ds] * (z * sigmoid(z))
        return sumsq + gated * gated, inner + gated * gm_ref[:, ds] * gain_ref[:, ds]

    zero = jnp.zeros((length, LANES), F32)
    sumsq, inner = lax.fori_loop(0, DI // LANES, sums, (zero, zero))
    scale = lax.rsqrt(jnp.sum(sumsq, axis=1, keepdims=True) / DI + EPSILON)
    coef = scale * scale * scale * (jnp.sum(inner, axis=1, keepdims=True) / DI)

    def conv_back(i, grad_act):
        ds = chunk_ds(i)
        wide = chunk_ds(i + DI // LANES)
        pre = pre_ref[:, ds]
        sg = sigmoid(pre)
        gpre = grad_act * (sg * (1.0 + pre * (1.0 - sg)))
        x = proj_ref[:, wide]
        total = cw_ref[KCONV - 1 : KCONV, ds] * gpre
        gconv_ref[KCONV : KCONV + 1, ds] = jnp.sum(gpre, axis=0, keepdims=True)
        gconv_ref[KCONV - 1 : KCONV, ds] = jnp.sum(gpre * x, axis=0, keepdims=True)
        for j in range(1, KCONV):
            live = gpre * shift_ref[:, j - 1 : j]
            back = pltpu.roll(live, length - j, 0)
            total = total + cw_ref[KCONV - 1 - j : KCONV - j, ds] * back
            gconv_ref[KCONV - 1 - j : KCONV - j, ds] = jnp.sum(back * x, axis=0, keepdims=True)
        glow_ref[:, wide] = total.astype(BF16)

    def pair(i, _):
        ds = chunk_ds(i)
        z = proj_ref[:, ds]
        sz = sigmoid(z)
        silu_z = z * sz
        scanned = scan_ref[:, ds]
        gated = scanned * silu_z
        grad_out = gm_ref[:, ds]
        gdi_ref[0:1, ds] = jnp.sum(grad_out * gated * scale, axis=0, keepdims=True)
        dgated = scale * (grad_out * gain_ref[:, ds]) - gated * coef
        dscan = dgated * silu_z
        glow_ref[:, ds] = (dgated * scanned * (sz * (1.0 + z * (1.0 - sz)))).astype(BF16)
        pre = pre_ref[:, ds]
        values = pre * sigmoid(pre)
        gdi_ref[1:2, ds] = jnp.sum(dscan * values, axis=0, keepdims=True)
        low = values.astype(BF16)
        dlow = dscan.astype(BF16)
        lane = lax.broadcasted_iota(jnp.int32, (length, LANES), 1)
        head_lane = lax.broadcasted_iota(jnp.int32, (length, LANES), 1)
        outs = []
        for side in range(2):
            h = 2 * i + side
            here = (lane < HDIM) if side == 0 else (lane >= HDIM)
            factor = decay_of(mask_s, run_s, runt_s, h)
            stept = stept_s[pl.ds(h, 1), :]
            inter = inter_s[...]
            scaled = factor * stept
            outs.append(dot(scaled * inter, dlow, TN))
            dweights = dot(jnp.where(here, dscan, 0.0), low, NT)
            dinter_s[...] += dweights * scaled
            pairs = dweights * factor * inter
            col_s[pl.ds(h, 1), :] = jnp.sum(pairs, axis=0, keepdims=True)
            row = jnp.sum(pairs * stept, axis=1, keepdims=True)
            row_s[...] += jnp.where(head_lane == h, row, 0.0)
        grad_values = jnp.where(lane < HDIM, outs[0], outs[1]) + skip_ref[:, ds] * dscan
        conv_back(i, grad_values)
        return 0

    lax.fori_loop(0, DI // LANES, pair, 0)
    dinter = dinter_s[...].astype(BF16)
    conv_back(DI // LANES, dot(dinter, queries, TN))
    conv_back(DI // LANES + 1, dot(dinter, keys))
    dstep = col_s[...].T
    drun = row_s[...] - dstep * step
    ddecay = lax.dot_general(
        mask_s[...], drun, TN, precision=HIGHEST, preferred_element_type=F32
    )
    dstep = dstep - ddecay * rate_ref[...]
    graw = dstep * sigmoid(shifted)
    graw_ref[...] = graw.astype(BF16)
    ghead_ref[0:1, :] = jnp.sum(graw, axis=0, keepdims=True)
    ghead_ref[1:2, :] = jnp.sum(ddecay * decay, axis=0, keepdims=True)


def forward_mixer(proj, raw, small):
    length = proj.shape[0]
    vec = pltpu.VMEM
    return pl.pallas_call(
        forward_kernel,
        out_shape=(
            jax.ShapeDtypeStruct((length, CONV), F32),
            jax.ShapeDtypeStruct((length, DI), F32),
            jax.ShapeDtypeStruct((length, DI), BF16),
        ),
        in_specs=[pl.BlockSpec(memory_space=vec)] * 10,
        out_specs=[pl.BlockSpec(memory_space=vec)] * 3,
        scratch_shapes=[
            pltpu.VMEM((length, length), F32),
            pltpu.VMEM((length, LANES), F32),
            pltpu.VMEM((LANES, length), F32),
            pltpu.VMEM((LANES, length), F32),
            pltpu.VMEM((length, length), F32),
            pltpu.VMEM((length, DI), F32),
        ],
        compiler_params=pltpu.CompilerParams(vmem_limit_bytes=40 * 2**20),
        cost_estimate=pl.CostEstimate(
            flops=HEADS * length * length * 280, bytes_accessed=length * 30000, transcendentals=0
        ),
        name="mixer_forward",
    )(proj, raw, *small)


def backward_mixer(proj, raw, small, pre, scanned, grad_mixer):
    length, width = proj.shape[0], DI + CONV
    vec = pltpu.VMEM
    return pl.pallas_call(
        backward_kernel,
        out_shape=(
            jax.ShapeDtypeStruct((length, width), BF16),
            jax.ShapeDtypeStruct((length, LANES), BF16),
            jax.ShapeDtypeStruct((8, CONV), F32),
            jax.ShapeDtypeStruct((8, DI), F32),
            jax.ShapeDtypeStruct((8, LANES), F32),
        ),
        in_specs=[pl.BlockSpec(memory_space=vec)] * 13,
        out_specs=[pl.BlockSpec(memory_space=vec)] * 5,
        scratch_shapes=[
            pltpu.VMEM((length, length), F32),
            pltpu.VMEM((length, LANES), F32),
            pltpu.VMEM((LANES, length), F32),
            pltpu.VMEM((LANES, length), F32),
            pltpu.VMEM((length, length), F32),
            pltpu.VMEM((length, length), F32),
            pltpu.VMEM((length, LANES), F32),
            pltpu.VMEM((LANES, length), F32),
        ],
        compiler_params=pltpu.CompilerParams(vmem_limit_bytes=40 * 2**20),
        cost_estimate=pl.CostEstimate(
            flops=HEADS * length * length * 800, bytes_accessed=length * 60000, transcendentals=0
        ),
        name="mixer_backward",
    )(proj, raw, *small, pre, scanned, grad_mixer)


def per_device(
    block_in,
    segment_ids,
    live_count,
    norm_gain,
    in_weight,
    conv_weight,
    conv_bias,
    step_bias,
    decay_log,
    skip_gain,
    gated_gain,
    out_weight,
    out_cotangent,
):
    devices = lax.axis_size("fsdp")
    length = block_in.shape[0]
    share, proj_width = in_weight.shape
    width = block_in.shape[1]
    smalls = jnp.concatenate(
        [norm_gain, conv_weight.T.reshape(-1), conv_bias, gated_gain]
    )
    small_cols = -(-smalls.shape[0] // share)
    fold = out_weight.size // share
    used = proj_width + fold + small_cols
    padded = -(-used // LANES) * LANES
    packed = jnp.concatenate(
        [
            out_weight.reshape(share, fold),
            in_weight,
            jnp.pad(smalls, (0, share * (padded - proj_width - fold) - smalls.shape[0])).reshape(
                share, padded - proj_width - fold
            ),
        ],
        axis=1,
    )
    everything = lax.all_gather(packed, "fsdp", axis=0, tiled=True)
    in_full = everything[:, fold : fold + proj_width]
    out_full = everything[:, :fold].reshape(devices * out_weight.shape[0], width)
    rest = everything[:, fold + proj_width :].reshape(devices, -1).astype(F32)
    a = norm_gain.shape[0]
    b = a + conv_weight.size
    c = b + conv_bias.shape[0]
    d = c + gated_gain.shape[0]
    gain_norm = rest[:, :a].reshape(-1)
    kernel_rows = jnp.moveaxis(rest[:, a:b].reshape(devices, KCONV, -1), 1, 0).reshape(KCONV, CONV)
    kernel_bias = rest[:, b:c].reshape(1, CONV)
    gated = rest[:, c:d].reshape(1, DI)
    conv_rows = jnp.concatenate([kernel_rows, kernel_bias, jnp.zeros((3, CONV), F32)], axis=0)

    def lanes(v):
        return jnp.pad(v, (0, LANES - v.shape[0])).reshape(1, LANES)

    slots = jnp.arange(length)
    shift = jnp.stack(
        [
            ((slots >= j) & (jnp.roll(segment_ids, j) == segment_ids)).astype(F32)
            for j in range(1, KCONV)
        ],
        axis=1,
    )
    shift = jnp.pad(shift, ((0, 0), (0, 8 - shift.shape[1])))
    small = (
        segment_ids.reshape(length, 1),
        segment_ids.reshape(1, length),
        shift,
        conv_rows,
        lanes(step_bias),
        lanes(jnp.exp(decay_log)),
        jnp.repeat(skip_gain, HDIM).reshape(1, DI),
        gated,
    )
    source = block_in.astype(F32)
    live_rows = (lax.iota(jnp.int32, length) < live_count[0]).astype(F32)
    masked = jnp.where(live_rows[:, None] > 0, out_cotangent, jnp.zeros_like(out_cotangent))
    normed = rms_scale(source, gain_norm).astype(BF16)
    main = DI + CONV
    projected = jnp.dot(normed, in_full[:, :main], preferred_element_type=F32)
    tail = jnp.pad(in_full[:, main:], ((0, 0), (0, LANES - HEADS)))
    raw = jnp.dot(normed, tail, preferred_element_type=F32)
    grad_mixer = lax.dot_general(masked, out_full, NT, preferred_element_type=F32)
    pre, scanned, mixer_low = forward_mixer(projected, raw, small)
    grad_out_w = lax.dot_general(mixer_low, masked, TN, preferred_element_type=F32)
    out_share = lax.psum_scatter(
        grad_out_w.astype(BF16), "fsdp", scatter_dimension=0, tiled=True
    ).astype(F32)
    branch = jnp.dot(mixer_low, out_full, preferred_element_type=F32)
    output = (source + live_rows[:, None] * branch).astype(BF16)
    glow, graw, gconv, gdi, ghead = backward_mixer(projected, raw, small, pre, scanned, grad_mixer)
    grad_low = jnp.concatenate([glow, graw], axis=1)
    grad_in_w = lax.dot_general(normed, grad_low, TN, preferred_element_type=F32)
    in_share = lax.optimization_barrier(
        lax.psum_scatter(grad_in_w.astype(BF16), "fsdp", scatter_dimension=0, tiled=True)
    )[:, :proj_width].astype(F32)
    grad_normed = lax.dot_general(glow, in_full[:, :main], NT, preferred_element_type=F32)
    grad_normed = grad_normed + lax.dot_general(graw, tail, NT, preferred_element_type=F32)
    _, norm_vjp = jax.vjp(rms_scale, source, gain_norm)
    grad_source, grad_gain = norm_vjp(grad_normed)
    grad_input = out_cotangent.astype(F32) + grad_source
    skip_part = gdi[1].reshape(HEADS, HDIM).sum(axis=1)
    heads = jnp.concatenate([ghead[0, :HEADS], ghead[1, :HEADS], skip_part])
    rows = jnp.concatenate(
        [
            grad_gain.reshape(devices, -1),
            jnp.moveaxis(gconv[:KCONV].reshape(KCONV, devices, -1), 0, 1).reshape(devices, -1),
            gconv[KCONV].reshape(devices, -1),
            gdi[0].reshape(devices, -1),
            jnp.broadcast_to(heads, (devices, heads.shape[0])),
        ],
        axis=1,
    )
    cols = -(-rows.shape[1] // LANES) * LANES
    rows = jnp.pad(rows, ((0, 0), (0, cols - rows.shape[1])))
    mine = lax.psum_scatter(rows, "fsdp", scatter_dimension=0, tiled=True)[0]
    head_sums = mine[d : d + 3 * HEADS].reshape(3, HEADS)
    return (
        output,
        grad_input,
        mine[:a],
        in_share,
        mine[a:b].reshape(KCONV, -1).T,
        mine[b:c],
        head_sums[0],
        head_sums[1],
        head_sums[2],
        mine[c:d],
        out_share,
    )


def solution(mesh):
    rows, vec, whole = P("fsdp", None), P("fsdp"), P()
    in_specs = (rows, vec, vec, vec, rows, rows, vec, whole, whole, whole, vec, rows, rows)
    out_specs = (rows, rows, vec, rows, rows, vec, whole, whole, whole, vec, rows)
    return jax.shard_map(
        per_device, mesh=mesh, in_specs=in_specs, out_specs=out_specs, check_vma=False
    )
```

```python
import functools

import jax
import jax.numpy as jnp
from jax import lax
from jax.experimental import pallas as pl
from jax.experimental.pallas import tpu as pltpu
from jax.sharding import PartitionSpec as P

DI = 1536
STATE = 128
HDIM = 64
KCONV = 4
HEADS = 24
CONV = 1792
LANES = 128
EPSILON = 1e-05
HIGHEST = lax.Precision.HIGHEST
F32 = jnp.float32
BF16 = jnp.bfloat16
NT = (((1,), (1,)), ((), ()))
TN = (((0,), (0,)), ((), ()))
MESH = pl.DeviceIdType.MESH


def rms_scale(values, gain_vec):
    return (
        values * lax.rsqrt(jnp.mean(values * values, axis=-1, keepdims=True) + EPSILON) * gain_vec
    )


def dot(a, b, dims=(((1,), (0,)), ((), ()))):
    return lax.dot_general(a.astype(BF16), b.astype(BF16), dims, preferred_element_type=F32)


def sigmoid(v):
    return 1.0 / (1.0 + jnp.exp(-v))


def softplus(v):
    return jnp.maximum(v, 0.0) + jnp.log1p(jnp.exp(-jnp.abs(v)))


def chunk_ds(i):
    return pl.ds(pl.multiple_of(i * LANES, LANES), LANES)


def head_prelude(raw_ref, segc, segr, bias_ref, rate_ref):
    length = raw_ref.shape[0]
    rows = lax.broadcasted_iota(jnp.int32, (length, length), 0)
    cols = lax.broadcasted_iota(jnp.int32, (length, length), 1)
    mask = ((rows >= cols) & (segc == segr)).astype(F32)
    shifted = raw_ref[...] + bias_ref[...]
    step = softplus(shifted)
    decay = -step * rate_ref[...]
    running = jnp.dot(mask, decay, precision=HIGHEST, preferred_element_type=F32)
    return mask, shifted, step, decay, running


def column(values, h):
    lane = lax.broadcasted_iota(jnp.int32, values.shape, 1)
    return jnp.sum(jnp.where(lane == h, values, 0.0), axis=1, keepdims=True)


def decay_of(mask_ref, run_ref, run_t_ref, h):
    spread = column(run_ref[...], h) - run_t_ref[pl.ds(h, 1), :]
    mask = mask_ref[...]
    return jnp.where(mask > 0, jnp.exp(jnp.where(mask > 0, spread, 0.0)), 0.0)


def forward_kernel(
    proj_ref, raw_ref, segc_ref, segr_ref, shift_ref, cw_ref, bias_ref, rate_ref, skip_ref, gain_ref,
    pre_ref, scan_ref, low_ref,
    mask_s, run_s, runt_s, stept_s, inter_s, gated_s,
):
    length = proj_ref.shape[0]
    mask, _, step, _, running = head_prelude(
        raw_ref, segc_ref[...], segr_ref[...], bias_ref, rate_ref
    )
    mask_s[...] = mask
    run_s[...] = running
    runt_s[...] = running.T
    stept_s[...] = step.T

    def conv(i, _):
        ds = chunk_ds(i)
        x = proj_ref[:, chunk_ds(i + DI // LANES)]
        total = cw_ref[KCONV : KCONV + 1, ds] + cw_ref[KCONV - 1 : KCONV, ds] * x
        for j in range(1, KCONV):
            moved = pltpu.roll(x, j, 0) * shift_ref[:, j - 1 : j]
            total = total + cw_ref[KCONV - 1 - j : KCONV - j, ds] * moved
        pre_ref[:, ds] = total
        return 0

    lax.fori_loop(0, CONV // LANES, conv, 0)
    pre_k = pre_ref[:, DI : DI + STATE]
    pre_q = pre_ref[:, DI + STATE :]
    inter_s[...] = dot(pre_q * sigmoid(pre_q), pre_k * sigmoid(pre_k), NT)

    def pair(i, sumsq):
        ds = chunk_ds(i)
        pre = pre_ref[:, ds]
        values = pre * sigmoid(pre)
        low = values.astype(BF16)
        outs = []
        for side in range(2):
            h = 2 * i + side
            weights = decay_of(mask_s, run_s, runt_s, h) * inter_s[...] * stept_s[pl.ds(h, 1), :]
            outs.append(dot(weights, low))
        lane = lax.broadcasted_iota(jnp.int32, (length, LANES), 1)
        scanned = jnp.where(lane < HDIM, outs[0], outs[1]) + skip_ref[:, ds] * values
        scan_ref[:, ds] = scanned
        z = proj_ref[:, ds]
        gated = scanned * (z * sigmoid(z))
        gated_s[:, ds] = gated
        return sumsq + gated * gated

    sumsq = lax.fori_loop(0, DI // LANES, pair, jnp.zeros((length, LANES), F32))
    scale = lax.rsqrt(jnp.sum(sumsq, axis=1, keepdims=True) / DI + EPSILON)

    def finish(i, _):
        ds = chunk_ds(i)
        low_ref[:, ds] = (gated_s[:, ds] * scale * gain_ref[:, ds]).astype(BF16)
        return 0

    lax.fori_loop(0, DI // LANES, finish, 0)


def backward_kernel(
    proj_ref, raw_ref, segc_ref, segr_ref, shift_ref, cw_ref, bias_ref, rate_ref, skip_ref, gain_ref,
    pre_ref, scan_ref, gm_ref,
    glow_ref, graw_ref, gconv_ref, gdi_ref, ghead_ref,
    mask_s, run_s, runt_s, stept_s, inter_s, dinter_s, row_s, col_s,
):
    length = proj_ref.shape[0]
    mask, shifted, step, decay, running = head_prelude(
        raw_ref, segc_ref[...], segr_ref[...], bias_ref, rate_ref
    )
    mask_s[...] = mask
    run_s[...] = running
    runt_s[...] = running.T
    stept_s[...] = step.T
    pre_k = pre_ref[:, DI : DI + STATE]
    pre_q = pre_ref[:, DI + STATE :]
    keys = (pre_k * sigmoid(pre_k)).astype(BF16)
    queries = (pre_q * sigmoid(pre_q)).astype(BF16)
    inter_s[...] = dot(queries, keys, NT)
    dinter_s[...] = jnp.zeros_like(dinter_s)
    row_s[...] = jnp.zeros_like(row_s)
    col_s[...] = jnp.zeros_like(col_s)
    gconv_ref[...] = jnp.zeros_like(gconv_ref)
    gdi_ref[...] = jnp.zeros_like(gdi_ref)
    ghead_ref[...] = jnp.zeros_like(ghead_ref)

    def sums(i, carry):
        sumsq, inner = carry
        ds = chunk_ds(i)
        z = proj_ref[:, ds]
        gated = scan_ref[:, ds] * (z * sigmoid(z))
        return sumsq + gated * gated, inner + gated * gm_ref[:, ds] * gain_ref[:, ds]

    zero = jnp.zeros((length, LANES), F32)
    sumsq, inner = lax.fori_loop(0, DI // LANES, sums, (zero, zero))
    scale = lax.rsqrt(jnp.sum(sumsq, axis=1, keepdims=True) / DI + EPSILON)
    coef = scale * scale * scale * (jnp.sum(inner, axis=1, keepdims=True) / DI)

    def conv_back(i, grad_act):
        ds = chunk_ds(i)
        wide = chunk_ds(i + DI // LANES)
        pre = pre_ref[:, ds]
        sg = sigmoid(pre)
        gpre = grad_act * (sg * (1.0 + pre * (1.0 - sg)))
        x = proj_ref[:, wide]
        total = cw_ref[KCONV - 1 : KCONV, ds] * gpre
        gconv_ref[KCONV : KCONV + 1, ds] = jnp.sum(gpre, axis=0, keepdims=True)
        gconv_ref[KCONV - 1 : KCONV, ds] = jnp.sum(gpre * x, axis=0, keepdims=True)
        for j in range(1, KCONV):
            live = gpre * shift_ref[:, j - 1 : j]
            back = pltpu.roll(live, length - j, 0)
            total = total + cw_ref[KCONV - 1 - j : KCONV - j, ds] * back
            gconv_ref[KCONV - 1 - j : KCONV - j, ds] = jnp.sum(back * x, axis=0, keepdims=True)
        glow_ref[:, wide] = total.astype(BF16)

    def pair(i, _):
        ds = chunk_ds(i)
        z = proj_ref[:, ds]
        sz = sigmoid(z)
        silu_z = z * sz
        scanned = scan_ref[:, ds]
        gated = scanned * silu_z
        grad_out = gm_ref[:, ds]
        gdi_ref[0:1, ds] = jnp.sum(grad_out * gated * scale, axis=0, keepdims=True)
        dgated = scale * (grad_out * gain_ref[:, ds]) - gated * coef
        dscan = dgated * silu_z
        glow_ref[:, ds] = (dgated * scanned * (sz * (1.0 + z * (1.0 - sz)))).astype(BF16)
        pre = pre_ref[:, ds]
        values = pre * sigmoid(pre)
        gdi_ref[1:2, ds] = jnp.sum(dscan * values, axis=0, keepdims=True)
        low = values.astype(BF16)
        dlow = dscan.astype(BF16)
        lane = lax.broadcasted_iota(jnp.int32, (length, LANES), 1)
        head_lane = lax.broadcasted_iota(jnp.int32, (length, LANES), 1)
        outs = []
        for side in range(2):
            h = 2 * i + side
            here = (lane < HDIM) if side == 0 else (lane >= HDIM)
            factor = decay_of(mask_s, run_s, runt_s, h)
            stept = stept_s[pl.ds(h, 1), :]
            inter = inter_s[...]
            scaled = factor * stept
            outs.append(dot(scaled * inter, dlow, TN))
            dweights = dot(jnp.where(here, dscan, 0.0), low, NT)
            dinter_s[...] += dweights * scaled
            pairs = dweights * factor * inter
            col_s[pl.ds(h, 1), :] = jnp.sum(pairs, axis=0, keepdims=True)
            row = jnp.sum(pairs * stept, axis=1, keepdims=True)
            row_s[...] += jnp.where(head_lane == h, row, 0.0)
        grad_values = jnp.where(lane < HDIM, outs[0], outs[1]) + skip_ref[:, ds] * dscan
        conv_back(i, grad_values)
        return 0

    lax.fori_loop(0, DI // LANES, pair, 0)
    dinter = dinter_s[...].astype(BF16)
    conv_back(DI // LANES, dot(dinter, queries, TN))
    conv_back(DI // LANES + 1, dot(dinter, keys))
    dstep = col_s[...].T
    drun = row_s[...] - dstep * step
    ddecay = lax.dot_general(
        mask_s[...], drun, TN, precision=HIGHEST, preferred_element_type=F32
    )
    dstep = dstep - ddecay * rate_ref[...]
    graw = dstep * sigmoid(shifted)
    graw_ref[...] = graw.astype(BF16)
    ghead_ref[0:1, :] = jnp.sum(graw, axis=0, keepdims=True)
    ghead_ref[1:2, :] = jnp.sum(ddecay * decay, axis=0, keepdims=True)


def forward_mixer(proj, raw, small):
    length = proj.shape[0]
    vec = pltpu.VMEM
    return pl.pallas_call(
        forward_kernel,
        out_shape=(
            jax.ShapeDtypeStruct((length, CONV), F32),
            jax.ShapeDtypeStruct((length, DI), F32),
            jax.ShapeDtypeStruct((length, DI), BF16),
        ),
        in_specs=[pl.BlockSpec(memory_space=vec)] * 10,
        out_specs=[pl.BlockSpec(memory_space=vec)] * 3,
        scratch_shapes=[
            pltpu.VMEM((length, length), F32),
            pltpu.VMEM((length, LANES), F32),
            pltpu.VMEM((LANES, length), F32),
            pltpu.VMEM((LANES, length), F32),
            pltpu.VMEM((length, length), F32),
            pltpu.VMEM((length, DI), F32),
        ],
        compiler_params=pltpu.CompilerParams(vmem_limit_bytes=40 * 2**20),
        cost_estimate=pl.CostEstimate(
            flops=HEADS * length * length * 280, bytes_accessed=length * 30000, transcendentals=0
        ),
        name="mixer_forward",
    )(proj, raw, *small)


def backward_mixer(proj, raw, small, pre, scanned, grad_mixer):
    length, width = proj.shape[0], DI + CONV
    vec = pltpu.VMEM
    return pl.pallas_call(
        backward_kernel,
        out_shape=(
            jax.ShapeDtypeStruct((length, width), BF16),
            jax.ShapeDtypeStruct((length, LANES), BF16),
            jax.ShapeDtypeStruct((8, CONV), F32),
            jax.ShapeDtypeStruct((8, DI), F32),
            jax.ShapeDtypeStruct((8, LANES), F32),
        ),
        in_specs=[pl.BlockSpec(memory_space=vec)] * 13,
        out_specs=[pl.BlockSpec(memory_space=vec)] * 5,
        scratch_shapes=[
            pltpu.VMEM((length, length), F32),
            pltpu.VMEM((length, LANES), F32),
            pltpu.VMEM((LANES, length), F32),
            pltpu.VMEM((LANES, length), F32),
            pltpu.VMEM((length, length), F32),
            pltpu.VMEM((length, length), F32),
            pltpu.VMEM((length, LANES), F32),
            pltpu.VMEM((LANES, length), F32),
        ],
        compiler_params=pltpu.CompilerParams(vmem_limit_bytes=40 * 2**20),
        cost_estimate=pl.CostEstimate(
            flops=HEADS * length * length * 800, bytes_accessed=length * 60000, transcendentals=0
        ),
        name="mixer_backward",
    )(proj, raw, *small, pre, scanned, grad_mixer)


def pair_barrier(me, half):
    core, chip = lax.rem(me, 2), lax.div(me, 2)
    partner = me + 1 - 2 * core
    barrier = pltpu.get_barrier_semaphore()
    pl.semaphore_signal(barrier, inc=1, device_id=(partner,), device_id_type=MESH)

    def greet(k, _):
        other = 2 * lax.rem(chip + 1 + k, half) + core
        pl.semaphore_signal(barrier, inc=1, device_id=(other,), device_id_type=MESH)
        return 0

    lax.fori_loop(0, half - 1, greet, 0)
    pl.semaphore_wait(barrier, half)
    return core, chip, partner


def loop(count, step):
    def body(k, _):
        step(k)
        return 0

    lax.fori_loop(0, count, body, 0)


def gather_kernel(
    n, x0, x1, x2, o0, o1, o2, own_sem, send_far, recv_far, send_near, recv_near
):
    half = n // 2
    me = lax.axis_index("fsdp")
    core, chip, partner = pair_barrier(me, half)
    groups = ((x0, o0), (x1, o1), (x2, o2))

    def far(g, k, slot):
        src, dst = groups[g]
        return pltpu.make_async_remote_copy(
            src_ref=src,
            dst_ref=dst.at[slot],
            send_sem=send_far.at[g, k],
            recv_sem=recv_far.at[g, k],
            device_id=(2 * lax.rem(chip + 1 + k, half) + core,),
            device_id_type=MESH,
        )

    def near(g, k, src, slot):
        return pltpu.make_async_remote_copy(
            src_ref=src,
            dst_ref=groups[g][1].at[slot],
            send_sem=send_near.at[g, k],
            recv_sem=recv_near.at[g, k],
            device_id=(partner,),
            device_id_type=MESH,
        )

    def origin(k):
        return 2 * lax.rem(chip + half - 1 - k, half)

    loop(half - 1, lambda k: [far(g, k, me).start() for g in range(3)] and None)
    for g in range(3):
        near(g, half - 1, groups[g][0], me).start()
        pltpu.make_async_copy(groups[g][0], groups[g][1].at[me], own_sem.at[g]).start()

    def forward(k):
        slot = origin(k) + core
        for g in range(3):
            far(g, k, slot).wait_recv()
            near(g, k, groups[g][1].at[slot], slot).start()

    loop(half - 1, forward)

    def drain(k):
        slot, other = origin(k) + core, origin(k) + 1 - core
        for g in range(3):
            near(g, k, groups[g][1].at[slot], other).wait_recv()
            near(g, k, groups[g][1].at[slot], slot).wait_send()
            far(g, k, me).wait_send()

    loop(half - 1, drain)
    for g in range(3):
        near(g, half - 1, groups[g][0], partner).wait_recv()
        near(g, half - 1, groups[g][0], me).wait_send()
        pltpu.make_async_copy(groups[g][0], groups[g][1].at[me], own_sem.at[g]).wait()


def reduce_kernel(
    n, a0, a1, a2, o0, o1, o2, p0, p1, p2, t0, t1, t2, q0, q1, q2,
    send_near, recv_near, send_far, recv_far,
):
    half = n // 2
    me = lax.axis_index("fsdp")
    core, chip, partner = pair_barrier(me, half)
    groups = ((a0, o0, p0, t0, q0), (a1, o1, p1, t1, q1), (a2, o2, p2, t2, q2))

    def target(k):
        return lax.rem(chip + 1 + k, half)

    def near(g, k):
        terms, _, got, _, _ = groups[g]
        return pltpu.make_async_remote_copy(
            src_ref=terms.at[2 * target(k) + 1 - core],
            dst_ref=got.at[k],
            send_sem=send_near.at[g, k],
            recv_sem=recv_near.at[g, k],
            device_id=(partner,),
            device_id_type=MESH,
        )

    def far(g, k):
        _, _, _, sums, got = groups[g]
        return pltpu.make_async_remote_copy(
            src_ref=sums.at[k],
            dst_ref=got.at[k],
            send_sem=send_far.at[g, k],
            recv_sem=recv_far.at[g, k],
            device_id=(2 * target(k) + core,),
            device_id_type=MESH,
        )

    def both(g, k):
        terms, _, got, _, _ = groups[g]
        near(g, k).wait_recv()
        return terms[2 * target(k) + core].astype(F32) + got[k].astype(F32)

    loop(half, lambda k: [near(g, k).start() for g in range(3)] and None)

    def pass_on(k):
        for g in range(3):
            sums = groups[g][3]
            sums[k] = both(g, k).astype(sums.dtype)

        @pl.when(k > 0)
        def _():
            for g in range(3):
                far(g, k - 1).start()

    loop(half - 1, pass_on)
    for g in range(3):
        groups[g][1][...] = both(g, half - 1)
    for g in range(3):
        far(g, half - 2).start()

    def collect(k):
        for g in range(3):
            far(g, k).wait_recv()
            groups[g][1][...] += groups[g][4][k].astype(F32)

    loop(half - 1, collect)

    def drain(k):
        for g in range(3):
            near(g, k).wait_send()

    def drain_far(k):
        for g in range(3):
            far(g, k).wait_send()

    loop(half, drain)
    loop(half - 1, drain_far)


def gather_all(n, shards):
    vmem = pl.BlockSpec(memory_space=pltpu.VMEM)
    half = n // 2
    return pl.pallas_call(
        functools.partial(gather_kernel, n),
        out_shape=tuple(jax.ShapeDtypeStruct((n,) + x.shape, x.dtype) for x in shards),
        in_specs=[vmem] * 3,
        out_specs=[vmem] * 3,
        scratch_shapes=[
            pltpu.SemaphoreType.DMA((3,)),
            pltpu.SemaphoreType.DMA((3, half)),
            pltpu.SemaphoreType.DMA((3, half)),
            pltpu.SemaphoreType.DMA((3, half)),
            pltpu.SemaphoreType.DMA((3, half)),
        ],
        compiler_params=pltpu.CompilerParams(
            collective_id=0, has_side_effects=True, vmem_limit_bytes=60 * 2**20
        ),
        name="gather_all",
    )(*shards)


def reduce_all(n, terms):
    vmem = pl.BlockSpec(memory_space=pltpu.VMEM)
    half = n // 2
    slots = [pltpu.VMEM((half,) + x.shape[1:], x.dtype) for x in terms]
    return pl.pallas_call(
        functools.partial(reduce_kernel, n),
        out_shape=tuple(jax.ShapeDtypeStruct(x.shape[1:], F32) for x in terms),
        in_specs=[vmem] * 3,
        out_specs=[vmem] * 3,
        scratch_shapes=slots * 3 + [pltpu.SemaphoreType.DMA((3, half))] * 4,
        compiler_params=pltpu.CompilerParams(
            collective_id=1, has_side_effects=True, vmem_limit_bytes=60 * 2**20
        ),
        name="reduce_all",
    )(*terms)


def per_device(
    block_in,
    segment_ids,
    live_count,
    norm_gain,
    in_weight,
    conv_weight,
    conv_bias,
    step_bias,
    decay_log,
    skip_gain,
    gated_gain,
    out_weight,
    out_cotangent,
):
    devices = lax.axis_size("fsdp")
    length = block_in.shape[0]
    share, proj_width = in_weight.shape
    width = block_in.shape[1]
    smalls = jnp.concatenate(
        [norm_gain, conv_weight.T.reshape(-1), conv_bias, gated_gain]
    )
    small_rows = -(-smalls.shape[0] // (8 * LANES)) * 8
    smalls = jnp.pad(smalls, (0, small_rows * LANES - smalls.shape[0])).reshape(small_rows, LANES)
    in_blocks, out_blocks, rest = gather_all(devices, (in_weight, out_weight, smalls))
    in_full = in_blocks.reshape(devices * share, proj_width)
    out_full = out_blocks.reshape(devices * out_weight.shape[0], width)
    rest = rest.reshape(devices, -1).astype(F32)
    a = norm_gain.shape[0]
    b = a + conv_weight.size
    c = b + conv_bias.shape[0]
    d = c + gated_gain.shape[0]
    gain_norm = rest[:, :a].reshape(-1)
    kernel_rows = jnp.moveaxis(rest[:, a:b].reshape(devices, KCONV, -1), 1, 0).reshape(KCONV, CONV)
    kernel_bias = rest[:, b:c].reshape(1, CONV)
    gated = rest[:, c:d].reshape(1, DI)
    conv_rows = jnp.concatenate([kernel_rows, kernel_bias, jnp.zeros((3, CONV), F32)], axis=0)

    def lanes(v):
        return jnp.pad(v, (0, LANES - v.shape[0])).reshape(1, LANES)

    slots = jnp.arange(length)
    shift = jnp.stack(
        [
            ((slots >= j) & (jnp.roll(segment_ids, j) == segment_ids)).astype(F32)
            for j in range(1, KCONV)
        ],
        axis=1,
    )
    shift = jnp.pad(shift, ((0, 0), (0, 8 - shift.shape[1])))
    small = (
        segment_ids.reshape(length, 1),
        segment_ids.reshape(1, length),
        shift,
        conv_rows,
        lanes(step_bias),
        lanes(jnp.exp(decay_log)),
        jnp.repeat(skip_gain, HDIM).reshape(1, DI),
        gated,
    )
    source = block_in.astype(F32)
    live_rows = (lax.iota(jnp.int32, length) < live_count[0]).astype(F32)
    masked = jnp.where(live_rows[:, None] > 0, out_cotangent, jnp.zeros_like(out_cotangent))
    normed = rms_scale(source, gain_norm).astype(BF16)
    main = DI + CONV
    projected = jnp.dot(normed, in_full[:, :main], preferred_element_type=F32)
    tail = jnp.pad(in_full[:, main:], ((0, 0), (0, LANES - HEADS)))
    raw = jnp.dot(normed, tail, preferred_element_type=F32)
    grad_mixer = lax.dot_general(masked, out_full, NT, preferred_element_type=F32)
    pre, scanned, mixer_low = forward_mixer(projected, raw, small)
    grad_out_w = lax.dot_general(mixer_low, masked, TN, preferred_element_type=F32)
    branch = jnp.dot(mixer_low, out_full, preferred_element_type=F32)
    output = (source + live_rows[:, None] * branch).astype(BF16)
    glow, graw, gconv, gdi, ghead = backward_mixer(projected, raw, small, pre, scanned, grad_mixer)
    grad_low = jnp.concatenate([glow, graw], axis=1)
    grad_in_w = lax.dot_general(normed, grad_low, TN, preferred_element_type=F32)
    grad_normed = lax.dot_general(glow, in_full[:, :main], NT, preferred_element_type=F32)
    grad_normed = grad_normed + lax.dot_general(graw, tail, NT, preferred_element_type=F32)
    _, norm_vjp = jax.vjp(rms_scale, source, gain_norm)
    grad_source, grad_gain = norm_vjp(grad_normed)
    grad_input = out_cotangent.astype(F32) + grad_source
    skip_part = gdi[1].reshape(HEADS, HDIM).sum(axis=1)
    heads = jnp.concatenate([ghead[0, :HEADS], ghead[1, :HEADS], skip_part])
    rows = jnp.concatenate(
        [
            grad_gain.reshape(devices, -1),
            jnp.moveaxis(gconv[:KCONV].reshape(KCONV, devices, -1), 0, 1).reshape(devices, -1),
            gconv[KCONV].reshape(devices, -1),
            gdi[0].reshape(devices, -1),
            jnp.broadcast_to(heads, (devices, heads.shape[0])),
        ],
        axis=1,
    )
    sum_rows = -(-rows.shape[1] // (8 * LANES)) * 8
    rows = jnp.pad(rows, ((0, 0), (0, sum_rows * LANES - rows.shape[1])))
    in_share, out_share, mine = reduce_all(
        devices,
        (
            grad_in_w.astype(BF16).reshape(devices, share, -1),
            grad_out_w.astype(BF16).reshape(devices, -1, width),
            rows.reshape(devices, sum_rows, LANES),
        ),
    )
    in_share = in_share[:, :proj_width]
    mine = mine.reshape(-1)
    head_sums = mine[d : d + 3 * HEADS].reshape(3, HEADS)
    return (
        output,
        grad_input,
        mine[:a],
        in_share,
        mine[a:b].reshape(KCONV, -1).T,
        mine[b:c],
        head_sums[0],
        head_sums[1],
        head_sums[2],
        mine[c:d],
        out_share,
    )


def solution(mesh):
    rows, vec, whole = P("fsdp", None), P("fsdp"), P()
    in_specs = (rows, vec, vec, vec, rows, rows, vec, whole, whole, whole, vec, rows, rows)
    out_specs = (rows, rows, vec, rows, rows, vec, whole, whole, whole, vec, rows)
    return jax.shard_map(
        per_device, mesh=mesh, in_specs=in_specs, out_specs=out_specs, check_vma=False
    )
```

```python
import functools

import jax
import jax.numpy as jnp
from jax import lax
from jax.experimental import pallas as pl
from jax.experimental.pallas import tpu as pltpu
from jax.sharding import PartitionSpec as P

DI = 1536
STATE = 128
HDIM = 64
KCONV = 4
HEADS = 24
CONV = 1792
LANES = 128
EPSILON = 1e-05
HIGHEST = lax.Precision.HIGHEST
F32 = jnp.float32
BF16 = jnp.bfloat16
NT = (((1,), (1,)), ((), ()))
TN = (((0,), (0,)), ((), ()))
MESH = pl.DeviceIdType.MESH


def rms_scale(values, gain_vec):
    return (
        values * lax.rsqrt(jnp.mean(values * values, axis=-1, keepdims=True) + EPSILON) * gain_vec
    )


def dot(a, b, dims=(((1,), (0,)), ((), ()))):
    return lax.dot_general(a.astype(BF16), b.astype(BF16), dims, preferred_element_type=F32)


def sigmoid(v):
    return 1.0 / (1.0 + jnp.exp(-v))


def softplus(v):
    return jnp.maximum(v, 0.0) + jnp.log1p(jnp.exp(-jnp.abs(v)))


def chunk_ds(i):
    return pl.ds(pl.multiple_of(i * LANES, LANES), LANES)


def head_prelude(raw_ref, segc, segr, bias_ref, rate_ref):
    length = raw_ref.shape[0]
    rows = lax.broadcasted_iota(jnp.int32, (length, length), 0)
    cols = lax.broadcasted_iota(jnp.int32, (length, length), 1)
    mask = ((rows >= cols) & (segc == segr)).astype(F32)
    shifted = raw_ref[...] + bias_ref[...]
    step = softplus(shifted)
    decay = -step * rate_ref[...]
    running = jnp.dot(mask, decay, precision=HIGHEST, preferred_element_type=F32)
    return mask, shifted, step, decay, running


def column(values, h):
    lane = lax.broadcasted_iota(jnp.int32, values.shape, 1)
    return jnp.sum(jnp.where(lane == h, values, 0.0), axis=1, keepdims=True)


def decay_of(mask_ref, run_ref, run_t_ref, h):
    spread = column(run_ref[...], h) - run_t_ref[pl.ds(h, 1), :]
    mask = mask_ref[...]
    return jnp.where(mask > 0, jnp.exp(jnp.where(mask > 0, spread, 0.0)), 0.0)


def forward_kernel(
    proj_ref, raw_ref, segc_ref, segr_ref, shift_ref, cw_ref, bias_ref, rate_ref, skip_ref, gain_ref,
    pre_ref, scan_ref, low_ref,
    mask_s, run_s, runt_s, stept_s, inter_s, gated_s,
):
    length = proj_ref.shape[0]
    mask, _, step, _, running = head_prelude(
        raw_ref, segc_ref[...], segr_ref[...], bias_ref, rate_ref
    )
    mask_s[...] = mask
    run_s[...] = running
    runt_s[...] = running.T
    stept_s[...] = step.T

    def conv(i, _):
        ds = chunk_ds(i)
        x = proj_ref[:, chunk_ds(i + DI // LANES)]
        total = cw_ref[KCONV : KCONV + 1, ds] + cw_ref[KCONV - 1 : KCONV, ds] * x
        for j in range(1, KCONV):
            moved = pltpu.roll(x, j, 0) * shift_ref[:, j - 1 : j]
            total = total + cw_ref[KCONV - 1 - j : KCONV - j, ds] * moved
        pre_ref[:, ds] = total
        return 0

    lax.fori_loop(0, CONV // LANES, conv, 0)
    pre_k = pre_ref[:, DI : DI + STATE]
    pre_q = pre_ref[:, DI + STATE :]
    inter_s[...] = dot(pre_q * sigmoid(pre_q), pre_k * sigmoid(pre_k), NT)

    def pair(i, sumsq):
        ds = chunk_ds(i)
        pre = pre_ref[:, ds]
        values = pre * sigmoid(pre)
        low = values.astype(BF16)
        outs = []
        for side in range(2):
            h = 2 * i + side
            weights = decay_of(mask_s, run_s, runt_s, h) * inter_s[...] * stept_s[pl.ds(h, 1), :]
            outs.append(dot(weights, low))
        lane = lax.broadcasted_iota(jnp.int32, (length, LANES), 1)
        scanned = jnp.where(lane < HDIM, outs[0], outs[1]) + skip_ref[:, ds] * values
        scan_ref[:, ds] = scanned
        z = proj_ref[:, ds]
        gated = scanned * (z * sigmoid(z))
        gated_s[:, ds] = gated
        return sumsq + gated * gated

    sumsq = lax.fori_loop(0, DI // LANES, pair, jnp.zeros((length, LANES), F32))
    scale = lax.rsqrt(jnp.sum(sumsq, axis=1, keepdims=True) / DI + EPSILON)

    def finish(i, _):
        ds = chunk_ds(i)
        low_ref[:, ds] = (gated_s[:, ds] * scale * gain_ref[:, ds]).astype(BF16)
        return 0

    lax.fori_loop(0, DI // LANES, finish, 0)


def backward_kernel(
    proj_ref, raw_ref, segc_ref, segr_ref, shift_ref, cw_ref, bias_ref, rate_ref, skip_ref, gain_ref,
    pre_ref, scan_ref, gm_ref,
    glow_ref, graw_ref, gconv_ref, gdi_ref, ghead_ref,
    mask_s, run_s, runt_s, stept_s, inter_s, dinter_s, row_s, col_s,
):
    length = proj_ref.shape[0]
    mask, shifted, step, decay, running = head_prelude(
        raw_ref, segc_ref[...], segr_ref[...], bias_ref, rate_ref
    )
    mask_s[...] = mask
    run_s[...] = running
    runt_s[...] = running.T
    stept_s[...] = step.T
    pre_k = pre_ref[:, DI : DI + STATE]
    pre_q = pre_ref[:, DI + STATE :]
    keys = (pre_k * sigmoid(pre_k)).astype(BF16)
    queries = (pre_q * sigmoid(pre_q)).astype(BF16)
    inter_s[...] = dot(queries, keys, NT)
    dinter_s[...] = jnp.zeros_like(dinter_s)
    row_s[...] = jnp.zeros_like(row_s)
    col_s[...] = jnp.zeros_like(col_s)
    gconv_ref[...] = jnp.zeros_like(gconv_ref)
    gdi_ref[...] = jnp.zeros_like(gdi_ref)
    ghead_ref[...] = jnp.zeros_like(ghead_ref)

    def sums(i, carry):
        sumsq, inner = carry
        ds = chunk_ds(i)
        z = proj_ref[:, ds]
        gated = scan_ref[:, ds] * (z * sigmoid(z))
        return sumsq + gated * gated, inner + gated * gm_ref[:, ds] * gain_ref[:, ds]

    zero = jnp.zeros((length, LANES), F32)
    sumsq, inner = lax.fori_loop(0, DI // LANES, sums, (zero, zero))
    scale = lax.rsqrt(jnp.sum(sumsq, axis=1, keepdims=True) / DI + EPSILON)
    coef = scale * scale * scale * (jnp.sum(inner, axis=1, keepdims=True) / DI)

    def conv_back(i, grad_act):
        ds = chunk_ds(i)
        wide = chunk_ds(i + DI // LANES)
        pre = pre_ref[:, ds]
        sg = sigmoid(pre)
        gpre = grad_act * (sg * (1.0 + pre * (1.0 - sg)))
        x = proj_ref[:, wide]
        total = cw_ref[KCONV - 1 : KCONV, ds] * gpre
        gconv_ref[KCONV : KCONV + 1, ds] = jnp.sum(gpre, axis=0, keepdims=True)
        gconv_ref[KCONV - 1 : KCONV, ds] = jnp.sum(gpre * x, axis=0, keepdims=True)
        for j in range(1, KCONV):
            live = gpre * shift_ref[:, j - 1 : j]
            back = pltpu.roll(live, length - j, 0)
            total = total + cw_ref[KCONV - 1 - j : KCONV - j, ds] * back
            gconv_ref[KCONV - 1 - j : KCONV - j, ds] = jnp.sum(back * x, axis=0, keepdims=True)
        glow_ref[:, wide] = total.astype(BF16)

    def pair(i, _):
        ds = chunk_ds(i)
        z = proj_ref[:, ds]
        sz = sigmoid(z)
        silu_z = z * sz
        scanned = scan_ref[:, ds]
        gated = scanned * silu_z
        grad_out = gm_ref[:, ds]
        gdi_ref[0:1, ds] = jnp.sum(grad_out * gated * scale, axis=0, keepdims=True)
        dgated = scale * (grad_out * gain_ref[:, ds]) - gated * coef
        dscan = dgated * silu_z
        glow_ref[:, ds] = (dgated * scanned * (sz * (1.0 + z * (1.0 - sz)))).astype(BF16)
        pre = pre_ref[:, ds]
        values = pre * sigmoid(pre)
        gdi_ref[1:2, ds] = jnp.sum(dscan * values, axis=0, keepdims=True)
        low = values.astype(BF16)
        dlow = dscan.astype(BF16)
        lane = lax.broadcasted_iota(jnp.int32, (length, LANES), 1)
        head_lane = lax.broadcasted_iota(jnp.int32, (length, LANES), 1)
        outs = []
        for side in range(2):
            h = 2 * i + side
            here = (lane < HDIM) if side == 0 else (lane >= HDIM)
            factor = decay_of(mask_s, run_s, runt_s, h)
            stept = stept_s[pl.ds(h, 1), :]
            inter = inter_s[...]
            scaled = factor * stept
            outs.append(dot(scaled * inter, dlow, TN))
            dweights = dot(jnp.where(here, dscan, 0.0), low, NT)
            dinter_s[...] += dweights * scaled
            pairs = dweights * factor * inter
            col_s[pl.ds(h, 1), :] = jnp.sum(pairs, axis=0, keepdims=True)
            row = jnp.sum(pairs * stept, axis=1, keepdims=True)
            row_s[...] += jnp.where(head_lane == h, row, 0.0)
        grad_values = jnp.where(lane < HDIM, outs[0], outs[1]) + skip_ref[:, ds] * dscan
        conv_back(i, grad_values)
        return 0

    lax.fori_loop(0, DI // LANES, pair, 0)
    dinter = dinter_s[...].astype(BF16)
    conv_back(DI // LANES, dot(dinter, queries, TN))
    conv_back(DI // LANES + 1, dot(dinter, keys))
    dstep = col_s[...].T
    drun = row_s[...] - dstep * step
    ddecay = lax.dot_general(
        mask_s[...], drun, TN, precision=HIGHEST, preferred_element_type=F32
    )
    dstep = dstep - ddecay * rate_ref[...]
    graw = dstep * sigmoid(shifted)
    graw_ref[...] = graw.astype(BF16)
    ghead_ref[0:1, :] = jnp.sum(graw, axis=0, keepdims=True)
    ghead_ref[1:2, :] = jnp.sum(ddecay * decay, axis=0, keepdims=True)


def forward_mixer(proj, raw, small):
    length = proj.shape[0]
    vec = pltpu.VMEM
    return pl.pallas_call(
        forward_kernel,
        out_shape=(
            jax.ShapeDtypeStruct((length, CONV), F32),
            jax.ShapeDtypeStruct((length, DI), F32),
            jax.ShapeDtypeStruct((length, DI), BF16),
        ),
        in_specs=[pl.BlockSpec(memory_space=vec)] * 10,
        out_specs=[pl.BlockSpec(memory_space=vec)] * 3,
        scratch_shapes=[
            pltpu.VMEM((length, length), F32),
            pltpu.VMEM((length, LANES), F32),
            pltpu.VMEM((LANES, length), F32),
            pltpu.VMEM((LANES, length), F32),
            pltpu.VMEM((length, length), F32),
            pltpu.VMEM((length, DI), F32),
        ],
        compiler_params=pltpu.CompilerParams(vmem_limit_bytes=40 * 2**20),
        cost_estimate=pl.CostEstimate(
            flops=HEADS * length * length * 280, bytes_accessed=length * 30000, transcendentals=0
        ),
        name="mixer_forward",
    )(proj, raw, *small)


def backward_mixer(proj, raw, small, pre, scanned, grad_mixer):
    length, width = proj.shape[0], DI + CONV
    vec = pltpu.VMEM
    return pl.pallas_call(
        backward_kernel,
        out_shape=(
            jax.ShapeDtypeStruct((length, width), BF16),
            jax.ShapeDtypeStruct((length, LANES), BF16),
            jax.ShapeDtypeStruct((8, CONV), F32),
            jax.ShapeDtypeStruct((8, DI), F32),
            jax.ShapeDtypeStruct((8, LANES), F32),
        ),
        in_specs=[pl.BlockSpec(memory_space=vec)] * 13,
        out_specs=[pl.BlockSpec(memory_space=vec)] * 5,
        scratch_shapes=[
            pltpu.VMEM((length, length), F32),
            pltpu.VMEM((length, LANES), F32),
            pltpu.VMEM((LANES, length), F32),
            pltpu.VMEM((LANES, length), F32),
            pltpu.VMEM((length, length), F32),
            pltpu.VMEM((length, length), F32),
            pltpu.VMEM((length, LANES), F32),
            pltpu.VMEM((LANES, length), F32),
        ],
        compiler_params=pltpu.CompilerParams(vmem_limit_bytes=40 * 2**20),
        cost_estimate=pl.CostEstimate(
            flops=HEADS * length * length * 800, bytes_accessed=length * 60000, transcendentals=0
        ),
        name="mixer_backward",
    )(proj, raw, *small, pre, scanned, grad_mixer)


def place(n):
    me = lax.axis_index("fsdp")
    core, chip = lax.rem(me, 2), lax.div(me, 2)
    plane, line = split(n)
    return me, core, lax.rem(chip, plane), lax.div(chip, plane)


def split(n):
    half = n // 2
    plane = 4 if half % 4 == 0 else 1
    return plane, half // plane


def loop(count, step):
    def body(k, _):
        step(k)
        return 0

    lax.fori_loop(0, count, body, 0)


def greet(n, me, core, spot, rank):
    plane, line = split(n)
    barrier = pltpu.get_barrier_semaphore()

    def signal(device):
        pl.semaphore_signal(barrier, inc=1, device_id=(device,), device_id_type=MESH)

    signal(me + 1 - 2 * core)
    for j in range(plane - 1):
        signal(2 * (rank * plane + lax.rem(spot + 1 + j, plane)) + core)
    loop(line - 1, lambda r: signal(2 * (lax.rem(rank + 1 + r, line) * plane + spot) + core))
    pl.semaphore_wait(barrier, plane + line - 1)


def gather_kernel(
    n, x0, x1, x2, o0, o1, o2, own_sem, s_line, r_line, s_plane, r_plane, s_near, r_near
):
    plane, line = split(n)
    me, core, spot, rank = place(n)
    partner = me + 1 - 2 * core
    greet(n, me, core, spot, rank)
    groups = ((x0, o0), (x1, o1), (x2, o2))

    def send(g, src, slot, sems, index, device):
        return pltpu.make_async_remote_copy(
            src_ref=src,
            dst_ref=groups[g][1].at[slot],
            send_sem=sems[0].at[g, index],
            recv_sem=sems[1].at[g, index],
            device_id=(device,),
            device_id_type=MESH,
        )

    def origin(r, j):
        from_rank = lax.rem(rank + 2 * line - 1 - r, line)
        return 2 * (from_rank * plane + lax.rem(spot + 2 * plane - 1 - j, plane))

    def along(g, r, slot):
        device = 2 * (lax.rem(rank + 1 + r, line) * plane + spot) + core
        return send(g, groups[g][0], slot, (s_line, r_line), r, device)

    def across(g, r, j, src, slot):
        device = 2 * (rank * plane + lax.rem(spot + 1 + j, plane)) + core
        return send(g, src, slot, (s_plane, r_plane), plane * r + j, device)

    def near(g, r, j, src, slot):
        return send(g, src, slot, (s_near, r_near), plane * r + j, partner)

    def start_along(r):
        for g in range(3):
            along(g, r, me).start()

    loop(line - 1, start_along)
    for g in range(3):
        x = groups[g][0]
        for j in range(plane - 1):
            across(g, line - 1, j, x, me).start()
        near(g, line - 1, plane - 1, x, me).start()
        pltpu.make_async_copy(x, groups[g][1].at[me], own_sem.at[g]).start()

    def forward(r):
        for j in range(plane - 1):
            slot = origin(r, j) + core
            for g in range(3):
                block = groups[g][1].at[slot]
                across(g, r, j, block, slot).wait_recv()
                near(g, r, j, block, slot).start()

    def spread(r):
        slot = origin(r, plane - 1) + core
        for g in range(3):
            block = groups[g][1].at[slot]
            along(g, r, slot).wait_recv()
            for j in range(plane - 1):
                across(g, r, j, block, slot).start()
            near(g, r, plane - 1, block, slot).start()
        forward(lax.rem(r + line - 1, line))

    loop(line - 1, spread)
    forward((line - 2) % line)

    def drain(r):
        for j in range(plane):
            slot, other = origin(r, j) + core, origin(r, j) + 1 - core
            for g in range(3):
                block = groups[g][1].at[slot]
                near(g, r, j, block, other).wait_recv()
                near(g, r, j, block, slot).wait_send()
                if j < plane - 1:
                    across(g, r, j, block, slot).wait_send()

    loop(line, drain)

    def drain_along(r):
        for g in range(3):
            along(g, r, me).wait_send()

    loop(line - 1, drain_along)
    for g in range(3):
        pltpu.make_async_copy(groups[g][0], groups[g][1].at[me], own_sem.at[g]).wait()


def reduce_kernel(
    n, a0, a1, a2, o0, o1, o2, p0, p1, p2, t0, t1, t2, q0, q1, q2,
    u0, u1, u2, v0, v1, v2, w0, w1, w2,
    s_near, r_near, s_plane, r_plane, s_line, r_line,
):
    plane, line = split(n)
    me, core, spot, rank = place(n)
    partner = me + 1 - 2 * core
    greet(n, me, core, spot, rank)
    groups = (
        (a0, o0, p0, t0, q0, u0, v0, w0),
        (a1, o1, p1, t1, q1, u1, v1, w1),
        (a2, o2, p2, t2, q2, u2, v2, w2),
    )

    def send(src, dst, sems, g, index, device):
        return pltpu.make_async_remote_copy(
            src_ref=src.at[index] if not isinstance(src, tuple) else src[0].at[src[1]],
            dst_ref=dst.at[index],
            send_sem=sems[0].at[g, index],
            recv_sem=sems[1].at[g, index],
            device_id=(device,),
            device_id_type=MESH,
        )

    def owner(r, j):
        return 2 * (lax.rem(rank + 1 + r, line) * plane + lax.rem(spot + 1 + j, plane))

    def near(g, r, j):
        src = (groups[g][0], owner(r, j) + 1 - core)
        return send(src, groups[g][2], (s_near, r_near), g, plane * r + j, partner)

    def across(g, r, j):
        device = 2 * (rank * plane + lax.rem(spot + 1 + j, plane)) + core
        return send(groups[g][3], groups[g][4], (s_plane, r_plane), g, plane * r + j, device)

    def along(g, r):
        device = 2 * (lax.rem(rank + 1 + r, line) * plane + spot) + core
        return send(groups[g][6], groups[g][7], (s_line, r_line), g, r, device)

    def both(g, r, j):
        near(g, r, j).wait_recv()
        return groups[g][0][owner(r, j) + core].astype(F32) + groups[g][2][plane * r + j].astype(F32)

    def start_near(r):
        for j in range(plane):
            for g in range(3):
                near(g, r, j).start()

    loop(line, start_near)

    def pairs(r):
        for j in range(plane):
            for g in range(3):
                if j < plane - 1:
                    sums = groups[g][3]
                    sums[plane * r + j] = both(g, r, j).astype(sums.dtype)
                else:
                    groups[g][5][r] = both(g, r, j)
            if j > 0:
                for g in range(3):
                    across(g, r, j - 1).start()

    def total(g, r):
        result = groups[g][5][r]
        for j in range(plane - 1):
            across(g, r, j).wait_recv()
            result = result + groups[g][4][plane * r + j].astype(F32)
        return result

    def planes(r):
        for g in range(3):
            sums = groups[g][6]
            sums[r] = total(g, r).astype(sums.dtype)
        for g in range(3):
            along(g, r).start()

    def step(r):
        pairs(r)

        @pl.when(r > 0)
        def _():
            planes(r - 1)

    loop(line, step)
    for g in range(3):
        groups[g][1][...] = total(g, line - 1)

    def collect(r):
        for g in range(3):
            along(g, r).wait_recv()
            groups[g][1][...] += groups[g][7][r].astype(F32)

    loop(line - 1, collect)

    def drain(r):
        for g in range(3):
            for j in range(plane):
                near(g, r, j).wait_send()
                if j < plane - 1:
                    across(g, r, j).wait_send()

    loop(line, drain)

    def drain_along(r):
        for g in range(3):
            along(g, r).wait_send()

    loop(line - 1, drain_along)


def gather_all(n, shards):
    vmem = pl.BlockSpec(memory_space=pltpu.VMEM)
    half, (_, line) = n // 2, split(n)
    return pl.pallas_call(
        functools.partial(gather_kernel, n),
        out_shape=tuple(jax.ShapeDtypeStruct((n,) + x.shape, x.dtype) for x in shards),
        in_specs=[vmem] * 3,
        out_specs=[vmem] * 3,
        scratch_shapes=[
            pltpu.SemaphoreType.DMA((3,)),
            pltpu.SemaphoreType.DMA((3, line)),
            pltpu.SemaphoreType.DMA((3, line)),
            pltpu.SemaphoreType.DMA((3, half)),
            pltpu.SemaphoreType.DMA((3, half)),
            pltpu.SemaphoreType.DMA((3, half)),
            pltpu.SemaphoreType.DMA((3, half)),
        ],
        compiler_params=pltpu.CompilerParams(
            collective_id=0, has_side_effects=True, vmem_limit_bytes=60 * 2**20
        ),
        name="gather_all",
    )(*shards)


def reduce_all(n, terms):
    vmem = pl.BlockSpec(memory_space=pltpu.VMEM)
    half, (_, line) = n // 2, split(n)
    slots = [pltpu.VMEM((half,) + x.shape[1:], x.dtype) for x in terms]
    partial_sums = [pltpu.VMEM((line,) + x.shape[1:], F32) for x in terms]
    lines = [pltpu.VMEM((line,) + x.shape[1:], x.dtype) for x in terms]
    return pl.pallas_call(
        functools.partial(reduce_kernel, n),
        out_shape=tuple(jax.ShapeDtypeStruct(x.shape[1:], F32) for x in terms),
        in_specs=[vmem] * 3,
        out_specs=[vmem] * 3,
        scratch_shapes=slots * 3
        + partial_sums
        + lines * 2
        + [pltpu.SemaphoreType.DMA((3, half))] * 4
        + [pltpu.SemaphoreType.DMA((3, line))] * 2,
        compiler_params=pltpu.CompilerParams(
            collective_id=1, has_side_effects=True, vmem_limit_bytes=60 * 2**20
        ),
        name="reduce_all",
    )(*terms)


def per_device(
    block_in,
    segment_ids,
    live_count,
    norm_gain,
    in_weight,
    conv_weight,
    conv_bias,
    step_bias,
    decay_log,
    skip_gain,
    gated_gain,
    out_weight,
    out_cotangent,
):
    devices = lax.axis_size("fsdp")
    length = block_in.shape[0]
    share, proj_width = in_weight.shape
    width = block_in.shape[1]
    smalls = jnp.concatenate(
        [norm_gain, conv_weight.T.reshape(-1), conv_bias, gated_gain]
    )
    small_rows = -(-smalls.shape[0] // (8 * LANES)) * 8
    smalls = jnp.pad(smalls, (0, small_rows * LANES - smalls.shape[0])).reshape(small_rows, LANES)
    in_blocks, out_blocks, rest = gather_all(devices, (in_weight, out_weight, smalls))
    in_full = in_blocks.reshape(devices * share, proj_width)
    out_full = out_blocks.reshape(devices * out_weight.shape[0], width)
    rest = rest.reshape(devices, -1).astype(F32)
    a = norm_gain.shape[0]
    b = a + conv_weight.size
    c = b + conv_bias.shape[0]
    d = c + gated_gain.shape[0]
    gain_norm = rest[:, :a].reshape(-1)
    kernel_rows = jnp.moveaxis(rest[:, a:b].reshape(devices, KCONV, -1), 1, 0).reshape(KCONV, CONV)
    kernel_bias = rest[:, b:c].reshape(1, CONV)
    gated = rest[:, c:d].reshape(1, DI)
    conv_rows = jnp.concatenate([kernel_rows, kernel_bias, jnp.zeros((3, CONV), F32)], axis=0)

    def lanes(v):
        return jnp.pad(v, (0, LANES - v.shape[0])).reshape(1, LANES)

    slots = jnp.arange(length)
    shift = jnp.stack(
        [
            ((slots >= j) & (jnp.roll(segment_ids, j) == segment_ids)).astype(F32)
            for j in range(1, KCONV)
        ],
        axis=1,
    )
    shift = jnp.pad(shift, ((0, 0), (0, 8 - shift.shape[1])))
    small = (
        segment_ids.reshape(length, 1),
        segment_ids.reshape(1, length),
        shift,
        conv_rows,
        lanes(step_bias),
        lanes(jnp.exp(decay_log)),
        jnp.repeat(skip_gain, HDIM).reshape(1, DI),
        gated,
    )
    source = block_in.astype(F32)
    live_rows = (lax.iota(jnp.int32, length) < live_count[0]).astype(F32)
    masked = jnp.where(live_rows[:, None] > 0, out_cotangent, jnp.zeros_like(out_cotangent))
    normed = rms_scale(source, gain_norm).astype(BF16)
    main = DI + CONV
    projected = jnp.dot(normed, in_full[:, :main], preferred_element_type=F32)
    tail = jnp.pad(in_full[:, main:], ((0, 0), (0, LANES - HEADS)))
    raw = jnp.dot(normed, tail, preferred_element_type=F32)
    grad_mixer = lax.dot_general(masked, out_full, NT, preferred_element_type=F32)
    pre, scanned, mixer_low = forward_mixer(projected, raw, small)
    grad_out_w = lax.dot_general(mixer_low, masked, TN, preferred_element_type=F32)
    branch = jnp.dot(mixer_low, out_full, preferred_element_type=F32)
    output = (source + live_rows[:, None] * branch).astype(BF16)
    glow, graw, gconv, gdi, ghead = backward_mixer(projected, raw, small, pre, scanned, grad_mixer)
    grad_low = jnp.concatenate([glow, graw], axis=1)
    grad_in_w = lax.dot_general(normed, grad_low, TN, preferred_element_type=F32)
    grad_normed = lax.dot_general(glow, in_full[:, :main], NT, preferred_element_type=F32)
    grad_normed = grad_normed + lax.dot_general(graw, tail, NT, preferred_element_type=F32)
    _, norm_vjp = jax.vjp(rms_scale, source, gain_norm)
    grad_source, grad_gain = norm_vjp(grad_normed)
    grad_input = out_cotangent.astype(F32) + grad_source
    skip_part = gdi[1].reshape(HEADS, HDIM).sum(axis=1)
    heads = jnp.concatenate([ghead[0, :HEADS], ghead[1, :HEADS], skip_part])
    rows = jnp.concatenate(
        [
            grad_gain.reshape(devices, -1),
            jnp.moveaxis(gconv[:KCONV].reshape(KCONV, devices, -1), 0, 1).reshape(devices, -1),
            gconv[KCONV].reshape(devices, -1),
            gdi[0].reshape(devices, -1),
            jnp.broadcast_to(heads, (devices, heads.shape[0])),
        ],
        axis=1,
    )
    sum_rows = -(-rows.shape[1] // (8 * LANES)) * 8
    rows = jnp.pad(rows, ((0, 0), (0, sum_rows * LANES - rows.shape[1])))
    in_share, out_share, mine = reduce_all(
        devices,
        (
            grad_in_w.astype(BF16).reshape(devices, share, -1),
            grad_out_w.astype(BF16).reshape(devices, -1, width),
            rows.reshape(devices, sum_rows, LANES),
        ),
    )
    in_share = in_share[:, :proj_width]
    mine = mine.reshape(-1)
    head_sums = mine[d : d + 3 * HEADS].reshape(3, HEADS)
    return (
        output,
        grad_input,
        mine[:a],
        in_share,
        mine[a:b].reshape(KCONV, -1).T,
        mine[b:c],
        head_sums[0],
        head_sums[1],
        head_sums[2],
        mine[c:d],
        out_share,
    )


def solution(mesh):
    rows, vec, whole = P("fsdp", None), P("fsdp"), P()
    in_specs = (rows, vec, vec, vec, rows, rows, vec, whole, whole, whole, vec, rows, rows)
    out_specs = (rows, rows, vec, rows, rows, vec, whole, whole, whole, vec, rows)
    return jax.shard_map(
        per_device, mesh=mesh, in_specs=in_specs, out_specs=out_specs, check_vma=False
    )
```
